32 devices in a mesh: blk: 8 (over z, x), head: 4 (over y, core).
Axes of the slice: x: 2, y: 2, z: 4, core: 2. Of those that a mesh axis runs over, the one named last changes fastest.
Arguments:
- ctx_q: bfloat16 [8192, 4096], P('blk', 'head'), may hold values from -120 to 120, as said below
- ctx_k: bfloat16 [8192, 1024], P('blk', 'head'), may hold values from -6 to 6
- ctx_v: bfloat16 [8192, 1024], P('blk', 'head'), may hold values from -6 to 6
- query_q: bfloat16 [8, 256, 4096], P('blk', None, 'head'), may hold values from -120 to 120, as said below
- query_k: bfloat16 [8, 256, 1024], P('blk', None, 'head'), may hold values from -6 to 6
- query_v: bfloat16 [8, 256, 1024], P('blk', None, 'head'), may hold values from -6 to 6
- out_weight: bfloat16 [4096, 4096], P('head', 'blk'), may hold values from -0.09375 to 0.09375
- anchor_index: int32 [1], replicated, may hold values from 0 to 7
- owner_index: int32 [1], replicated, may hold values from 0 to 7
- counts: int32 [8], replicated, may hold values from 256 to 1024, as said below
Outputs:
- ctx_out: bfloat16 [8192, 4096], P('blk', 'head')
- answer: bfloat16 [256, 4096], P(None, 'blk')
The draws below stay inside these ranges and needn't reach their ends.
Inputs may be any that keep to these rules, and one draw needn't show every extreme that they name: `ctx_q`: row 5 mod 64 of a block or query slab may be a large multiple of a key row of the same head nearby. `query_q`: row 5 mod 64 of a slab may be a large multiple of a key row of the same head nearby. `counts`: some block has exactly 1024 valid tokens.
All inputs are finite; a program needn't handle non-finite values.
Results may differ from the reference program's by a relative error of at most 0.0056.
Values may be sent and summed in bfloat16 or wider, within the bound.
No kernel may reach another device: no remote copies, remote signals or barrier semaphores. Data moves between devices by JAX's collectives and lax.ppermute only.
A program may use at most 128 MiB of HBM per device.

```python
import jax
import jax.numpy as jnp
from jax import lax

D = 4096
HEADS = 32
KV_HEADS = 8
HEAD_DIM = 128
BLOCK = 1024
QT = 256
CTX = 8192
N_BLK = 8


def shaped_pair(key, lead):
    group = HEADS // KV_HEADS
    keys = jnp.clip(jax.random.normal(jax.random.fold_in(key, 11), lead + (KV_HEADS, HEAD_DIM), jnp.float32), -6.0, 6.0)
    queries = jnp.clip(jax.random.normal(jax.random.fold_in(key, 12), lead + (KV_HEADS, group, HEAD_DIM), jnp.float32), -6.0, 6.0)
    return (queries.reshape(lead + (HEADS * HEAD_DIM,)).astype(jnp.bfloat16), keys.reshape(lead + (KV_HEADS * HEAD_DIM,)).astype(jnp.bfloat16))


def draw_ctx_q(key, part):
    return shaped_pair(key, (CTX,))[0]


def draw_ctx_k(key, part):
    return shaped_pair(key, (CTX,))[1]


def draw_query_q(key, part):
    return shaped_pair(jax.random.fold_in(key, 21), (N_BLK, QT))[0]


def draw_query_k(key, part):
    return shaped_pair(jax.random.fold_in(key, 21), (N_BLK, QT))[1]


def draw_counts(key, part):
    values = jax.random.randint(jax.random.fold_in(key, 31), (N_BLK,), BLOCK // 4, BLOCK + 1)
    full_block = jax.random.randint(jax.random.fold_in(key, 32), (), 0, N_BLK)
    return values.at[full_block].set(BLOCK).astype(jnp.int32)


def shard_levels(own_key, extent, shards, smallest, largest):
    def one(dim, shards_of):
        heights = jax.random.uniform(jax.random.fold_in(jax.random.fold_in(own_key, 6), dim), (shards_of,), jnp.float32, smallest / len(shards), largest / len(shards))
        return jnp.repeat(jnp.exp(heights), extent[dim] // shards_of).reshape((-1,) + (1,) * (len(extent) - dim - 1))

    loudness = one(*shards[0])
    for cut in shards[1:]:
        loudness = loudness * one(*cut)
    return loudness


def bell_draw(key, shape, spread, bound, pieces=(), kind=jnp.bfloat16):
    factor_of = shard_levels(key, shape, pieces, -0.22, 0.18) if pieces else 1.0
    values = jax.random.normal(key, shape, jnp.float32) * spread * factor_of
    return jnp.minimum(jnp.maximum(values, -bound), bound).astype(kind)


def setup_inputs(seed: int = 0) -> dict:
    streams_of = jax.random.split(jax.random.key(seed), 11)
    ctx_q = draw_ctx_q(jax.random.fold_in(streams_of[10], 71), 0)
    ctx_k = draw_ctx_k(jax.random.fold_in(streams_of[10], 71), 0)
    ctx_v = bell_draw(streams_of[2], (CTX, KV_HEADS * HEAD_DIM), 1.0, 6.0, ((0, 8), (1, 4)))
    query_q = draw_query_q(jax.random.fold_in(streams_of[10], 71), 0)
    query_k = draw_query_k(jax.random.fold_in(streams_of[10], 71), 0)
    query_v = bell_draw(streams_of[5], (N_BLK, QT, KV_HEADS * HEAD_DIM), 1.0, 6.0, ((0, 8), (2, 4)))
    out_weight = bell_draw(streams_of[6], (HEADS * HEAD_DIM, D), (HEADS * HEAD_DIM) ** -0.5, 0.09375, ((0, 4), (1, 8)))
    anchor_index = jax.random.randint(streams_of[7], (1,), 0, N_BLK).astype(jnp.int32)
    owner_index = jax.random.randint(streams_of[8], (1,), 0, N_BLK).astype(jnp.int32)
    counts = draw_counts(jax.random.fold_in(streams_of[10], 71), 0)
    return dict(ctx_q=ctx_q, ctx_k=ctx_k, ctx_v=ctx_v, query_q=query_q, query_k=query_k, query_v=query_v, out_weight=out_weight, anchor_index=anchor_index, owner_index=owner_index, counts=counts)


def attend(queries, keys, values, mask):
    scale = HEAD_DIM ** -0.5
    qh = queries.transpose(1, 0, 2, 3)
    kh = keys.transpose(1, 0, 2)
    vh = values.transpose(1, 0, 2)

    def one_head(item):
        qa, ka, va = item
        scores = jnp.einsum('rgd,kd->grk', qa.astype(jnp.float32), ka.astype(jnp.float32)) * scale
        scores = jnp.where(mask[None], scores, -1e30)
        top = jnp.max(scores, axis=-1)
        weights = jnp.where(mask[None], jnp.exp(scores - top[..., None]), 0.0)
        total = jnp.sum(weights, axis=-1)
        rounded = weights.astype(jnp.bfloat16).astype(jnp.float32)
        summed = jnp.einsum('grk,kd->grd', rounded, va.astype(jnp.float32))
        return top, total, summed

    return lax.map(one_head, (qh, kh, vh))


def combine(first, second):
    ma, la, oa = first
    mb, lb, ob = second
    top = jnp.maximum(ma, mb)
    ea = jnp.exp(ma - top)
    eb = jnp.exp(mb - top)
    return top, la * ea + lb * eb, oa * ea[..., None] + ob * eb[..., None]


def reference(ctx_q, ctx_k, ctx_v, query_q, query_k, query_v, out_weight, anchor_index, owner_index, counts):
    group = HEADS // KV_HEADS
    qb = ctx_q.reshape(N_BLK, BLOCK, KV_HEADS, group, HEAD_DIM)
    kb = ctx_k.reshape(N_BLK, BLOCK, KV_HEADS, HEAD_DIM)
    vb = ctx_v.reshape(N_BLK, BLOCK, KV_HEADS, HEAD_DIM)
    anchor = anchor_index[0]
    owner = owner_index[0]
    anchor_count = counts[anchor]
    row_pos = jnp.arange(BLOCK, dtype=jnp.int32)[:, None]
    col = jnp.arange(2 * BLOCK, dtype=jnp.int32)[None, :]
    inner = col - BLOCK

    def phase_one(index):
        own_count = counts[index]
        keys = jnp.concatenate([kb[anchor], kb[index]], axis=0)
        values = jnp.concatenate([vb[anchor], vb[index]], axis=0)
        mask = jnp.where(col < BLOCK, (col < anchor_count) & (index != anchor),
                         (inner <= row_pos) & (inner < own_count))
        top, total, summed = attend(qb[index], keys, values, mask)
        normed = summed / total[..., None]
        out = normed.transpose(2, 0, 1, 3).reshape(BLOCK, HEADS * HEAD_DIM)
        return jnp.where(row_pos < own_count, out, 0.0).astype(jnp.bfloat16)

    ctx_out = lax.map(phase_one, jnp.arange(N_BLK, dtype=jnp.int32)).reshape(CTX, HEADS * HEAD_DIM)

    query = query_q[owner].reshape(QT, KV_HEADS, group, HEAD_DIM)
    own_keys = query_k[owner].reshape(QT, KV_HEADS, HEAD_DIM)
    own_values = query_v[owner].reshape(QT, KV_HEADS, HEAD_DIM)
    qpos = jnp.arange(QT, dtype=jnp.int32)[:, None]
    col2 = jnp.arange(BLOCK + QT, dtype=jnp.int32)[None, :]
    inner2 = col2 - BLOCK

    def phase_two(carry, index):
        keys = jnp.concatenate([kb[index], own_keys], axis=0)
        values = jnp.concatenate([vb[index], own_values], axis=0)
        mask = jnp.where(col2 < BLOCK, col2 < counts[index], (inner2 <= qpos) & (index == owner))
        part = attend(query, keys, values, mask)
        return combine(carry, part), None

    start = (jnp.full((KV_HEADS, group, QT), -1e30, jnp.float32),
             jnp.zeros((KV_HEADS, group, QT), jnp.float32),
             jnp.zeros((KV_HEADS, group, QT, HEAD_DIM), jnp.float32))
    (top, total, summed), _ = lax.scan(phase_two, start, jnp.arange(N_BLK, dtype=jnp.int32))
    attn = (summed / total[..., None]).transpose(2, 0, 1, 3).reshape(QT, HEADS * HEAD_DIM).astype(jnp.bfloat16)
    answer = jnp.dot(attn, out_weight, preferred_element_type=jnp.float32).astype(jnp.bfloat16)
    return ctx_out, answer
```

```python
import functools
import math

import jax
import jax.numpy as jnp
from jax import lax
from jax.experimental import pallas as pl
from jax.experimental.pallas import tpu as pltpu
from jax.sharding import PartitionSpec as P

HEADS = 32
KV_HEADS = 8
GROUP = HEADS // KV_HEADS
HD = 128
C = HD**-0.5 * math.log2(math.e)
NEG = -1e30
NT = (((1,), (1,)), ((), ()))
TM = 256


def code_of(i):
    u = i >> 1
    return (i & 1) | ((u ^ (u >> 1)) << 1)


def partner_pairs(n, bit):
    back = {code_of(i): i for i in range(n)}
    return [(i, back[code_of(i) ^ (1 << bit)]) for i in range(n)]


def log2_of(n):
    k = n.bit_length() - 1
    assert 1 << k == n
    return k


def swap(value, axis, n, bit):
    return lax.ppermute(value, axis, partner_pairs(n, bit))


def spans(total, parts, unit):
    units = total // unit
    out, at = [], 0
    for p in range(parts):
        size = (units - at) // (parts - p) + (1 if (units - at) % (parts - p) else 0)
        out.append((at * unit, (at + size) * unit))
        at += size
    return [s for s in out if s[1] > s[0]]


def scores(q, k):
    return lax.dot_general(q, k, NT, preferred_element_type=jnp.float32)


def lane_max(s):
    m = s[:, :128]
    for j in range(1, s.shape[1] // 128):
        m = jnp.maximum(m, s[:, j * 128 : (j + 1) * 128])
    return jnp.max(m, axis=1, keepdims=True)


def weigh(p, v):
    wide = jnp.concatenate([v, jnp.ones_like(v)], axis=1)
    both = jnp.dot(p.astype(jnp.bfloat16), wide, preferred_element_type=jnp.float32)
    return both


def attend(s_parts, v_parts):
    m = functools.reduce(jnp.maximum, [lane_max(s) for s in s_parts])
    mc = m * C
    acc = None
    for s, v in zip(s_parts, v_parts):
        both = weigh(jnp.exp2(s * C - mc), v)
        acc = both if acc is None else acc + both
    return m, acc[:, HD:], acc[:, :HD]


def causal(n, width, first_col):
    r = lax.broadcasted_iota(jnp.int32, (n, width), 0)
    c = lax.broadcasted_iota(jnp.int32, (n, width), 1) + first_col
    return c <= r


def own_kernel(q_ref, k_ref, v_ref, o_ref, m_ref, l_ref):
    rows = q_ref.shape[0]
    h = pl.program_id(0)
    lane = lax.broadcasted_iota(jnp.int32, (TM, 128), 1)
    for i in range(rows // TM):
        at = pl.ds(i * TM, TM)
        q = q_ref[at, :]
        n = i * TM
        s_parts = [jnp.where(causal(TM, TM, 0), scores(q, k_ref[at, :]), NEG)]
        v_parts = [v_ref[at, :]]
        if n:
            s_parts.append(scores(q, k_ref[:n, :]))
            v_parts.append(v_ref[:n, :])
        m, total, o = attend(s_parts, v_parts)
        o_ref[at, :] = o
        m_ref[at, :] = jnp.where(lane == h, m, m_ref[at, :])
        l_ref[at, :] = jnp.where(lane == h, total, l_ref[at, :])


def own_call(q, k, v, lo, hi):
    rows = q.shape[0]
    n = hi - lo
    f32 = jnp.float32
    stat = pl.BlockSpec((rows, 128), lambda h: (0, 0))
    return pl.pallas_call(
        own_kernel,
        grid=(n,),
        in_specs=[
            pl.BlockSpec((rows, HD), lambda h: (0, lo + h)),
            pl.BlockSpec((rows, HD), lambda h: (0, (lo + h) // GROUP)),
            pl.BlockSpec((rows, HD), lambda h: (0, (lo + h) // GROUP)),
        ],
        out_specs=[pl.BlockSpec((rows, HD), lambda h: (0, h)), stat, stat],
        out_shape=[
            jax.ShapeDtypeStruct((rows, n * HD), f32),
            jax.ShapeDtypeStruct((rows, 128), f32),
            jax.ShapeDtypeStruct((rows, 128), f32),
        ],
        compiler_params=pltpu.CompilerParams(vmem_limit_bytes=40 << 20),
        cost_estimate=pl.CostEstimate(
            flops=n * rows * rows * HD * 5, bytes_accessed=n * rows * HD * 10, transcendentals=0
        ),
        name="own",
    )(q, k, v)


def pick(ref, at, lane, h):
    return jnp.max(jnp.where(lane == h, ref[at, :], NEG), axis=1, keepdims=True)


def anchor_kernel(bounds, lo, n_ref, q_ref, *refs):
    parts = len(bounds)
    k_refs, v_refs = refs[:parts], refs[parts : 2 * parts]
    o_ref, m_ref, l_ref, _, out_ref = refs[2 * parts :]
    rows = q_ref.shape[0]
    h = pl.program_id(0)
    lane = lax.broadcasted_iota(jnp.int32, (TM, 128), 1)
    bias = [
        jnp.where(lax.broadcasted_iota(jnp.int32, (1, b - a), 1) + a < n_ref[0], 0.0, NEG)
        for a, b in bounds
    ]
    for i in range(rows // TM):
        at = pl.ds(i * TM, TM)
        q = q_ref[at, :]
        s_parts = [scores(q, k[...]) + b for k, b in zip(k_refs, bias)]
        m, total, o = attend(s_parts, [v[...] for v in v_refs])
        m_own, l_own = pick(m_ref, at, lane, h), pick(l_ref, at, lane, h)
        top = jnp.maximum(m, m_own)
        wa, wb = jnp.exp2((m - top) * C), jnp.exp2((m_own - top) * C)
        normed = (o * wa + o_ref[at, :] * wb) / (total * wa + l_own * wb)
        row = lax.broadcasted_iota(jnp.int32, (TM, 128), 0) + i * TM
        out_ref[at, :] = jnp.where(row < n_ref[1], normed, 0.0).astype(out_ref.dtype)


def anchor_call(limits, q, kv_parts, bounds, own, out, lo, hi):
    rows = q.shape[0]
    n = hi - lo
    kv = kv_parts[0].shape[1] // (2 * HD)
    stat = pl.BlockSpec((rows, 128), lambda h, _: (0, 0))
    k_specs = [pl.BlockSpec((b - a, HD), lambda h, _: (0, (lo + h) // GROUP)) for a, b in bounds]
    v_specs = [
        pl.BlockSpec((b - a, HD), lambda h, _: (0, kv + (lo + h) // GROUP)) for a, b in bounds
    ]
    o, m, l = own
    in_specs = [
        pl.BlockSpec((rows, HD), lambda h, _: (0, lo + h)),
        *k_specs,
        *v_specs,
        pl.BlockSpec((rows, HD), lambda h, _: (0, h)),
        stat,
        stat,
    ]
    operands = [limits, q, *kv_parts, *kv_parts, o, m, l]
    aliases = {}
    in_specs.append(pl.BlockSpec(memory_space=pl.ANY))
    if out is None:
        operands.append(q)
    else:
        operands.append(out)
        aliases = {len(operands) - 1: 0}
    return pl.pallas_call(
        functools.partial(anchor_kernel, bounds, lo),
        grid_spec=pltpu.PrefetchScalarGridSpec(
            num_scalar_prefetch=1,
            grid=(n,),
            in_specs=in_specs,
            out_specs=pl.BlockSpec((rows, HD), lambda h, _: (0, lo + h)),
        ),
        out_shape=jax.ShapeDtypeStruct(q.shape, q.dtype),
        input_output_aliases=aliases,
        compiler_params=pltpu.CompilerParams(vmem_limit_bytes=40 << 20),
        cost_estimate=pl.CostEstimate(
            flops=n * rows * rows * HD * 8, bytes_accessed=n * rows * HD * 10, transcendentals=0
        ),
        name="anchor",
    )(*operands)


def split3(x):
    hi = x.astype(jnp.bfloat16).astype(jnp.float32)
    mid = (x - hi).astype(jnp.bfloat16).astype(jnp.float32)
    return hi, mid, x - hi - mid


def store_stat(ref, values):
    rows = values[0].shape[0]
    lane = lax.broadcasted_iota(jnp.int32, (rows, 128), 1)
    out = jnp.zeros((rows, 128), jnp.float32)
    for h, x in enumerate(values):
        for t, y in enumerate(split3(x)):
            out = jnp.where(lane == 3 * h + t, y, out)
    ref[...] = out.astype(ref.dtype)


def load_stat(block, h):
    x = block.astype(jnp.float32)
    lane = lax.broadcasted_iota(jnp.int32, x.shape, 1)
    keep = (lane >= 3 * h) & (lane < 3 * h + 3)
    return jnp.sum(jnp.where(keep, x, 0.0), axis=1, keepdims=True)


def query_kernel(heads, lo, n_ref, q_ref, k_ref, v_ref, k2_ref, v2_ref, out_ref):
    rows, keys = q_ref.shape[0], k_ref.shape[0]
    bias = jnp.where(lax.broadcasted_iota(jnp.int32, (1, keys), 1) < n_ref[0], 0.0, NEG)
    seen = causal(rows, rows, 0) & (n_ref[1] > 0)
    lses = []
    for h in range(heads):
        cols = slice(h * HD, (h + 1) * HD)
        g = (lo + h) // GROUP
        at = slice(g * HD, (g + 1) * HD)
        q = q_ref[:, cols]
        s_parts = [
            scores(q, k_ref[:, at]) + bias,
            jnp.where(seen, scores(q, k2_ref[0, :, at]), NEG),
        ]
        m, total, o = attend(s_parts, [v_ref[:, at], v2_ref[0, :, at]])
        out_ref[:, cols] = (o / total).astype(out_ref.dtype)
        lses.append(m * C + jnp.log2(total[:, :1]))
    store_stat(out_ref.at[:, heads * HD :], lses)


def query_call(limits, q, k, v, k2, v2, lo, hi):
    rows = q.shape[0]
    n = hi - lo
    vmem = pl.BlockSpec(memory_space=pltpu.VMEM)
    return pl.pallas_call(
        functools.partial(query_kernel, n, lo),
        in_specs=[pl.BlockSpec(memory_space=pltpu.SMEM)] + [vmem] * 5,
        out_specs=vmem,
        out_shape=jax.ShapeDtypeStruct((rows, n * HD + 128), jnp.bfloat16),
        compiler_params=pltpu.CompilerParams(vmem_limit_bytes=40 << 20),
        cost_estimate=pl.CostEstimate(
            flops=n * rows * (k.shape[0] + rows) * HD * 8,
            bytes_accessed=rows * n * HD * 4,
            transcendentals=0,
        ),
        name="query",
    )(limits, q, k, v, k2, v2)


def merged(a_ref, b_ref, h, heads):
    cols = slice(h * HD, (h + 1) * HD)
    la, lb = load_stat(a_ref[:, heads * HD :], h), load_stat(b_ref[:, heads * HD :], h)
    top = jnp.maximum(la, lb)
    wa, wb = jnp.exp2(la - top), jnp.exp2(lb - top)
    both = wa + wb
    o = a_ref[:, cols].astype(jnp.float32) * (wa / both) + b_ref[:, cols].astype(jnp.float32) * (
        wb / both
    )
    return o, top + jnp.log2(both)


def merge_kernel(widths, *refs):
    n = len(widths)
    for a, b, out, heads in zip(refs[:n], refs[n : 2 * n], refs[2 * n :], widths):
        lses = []
        for h in range(heads):
            o, lse = merged(a, b, h, heads)
            out[:, h * HD : (h + 1) * HD] = o.astype(out.dtype)
            lses.append(lse)
        store_stat(out.at[:, heads * HD :], lses)


def merge_call(mine, other, widths):
    vmem = pl.BlockSpec(memory_space=pltpu.VMEM)
    return pl.pallas_call(
        functools.partial(merge_kernel, widths),
        in_specs=[vmem] * (2 * len(widths)),
        out_specs=[vmem] * len(widths),
        out_shape=[jax.ShapeDtypeStruct(a.shape, a.dtype) for a in mine],
        cost_estimate=pl.CostEstimate(flops=1 << 20, bytes_accessed=3 << 20, transcendentals=0),
        name="merge",
    )(*mine, *other)


def project_kernel(widths, w_ref, *refs):
    n = len(widths)
    out_ref = refs[2 * n]
    acc, at = None, 0
    for a, b, heads in zip(refs[:n], refs[n : 2 * n], widths):
        o = jnp.concatenate(
            [merged(a, b, h, heads)[0].astype(jnp.bfloat16) for h in range(heads)], axis=1
        )
        part = jnp.dot(o, w_ref[at : at + heads * HD, :], preferred_element_type=jnp.float32)
        acc = part if acc is None else acc + part
        at += heads * HD
    out_ref[...] = acc.astype(out_ref.dtype)


def project_call(mine, other, widths, w):
    vmem = pl.BlockSpec(memory_space=pltpu.VMEM)
    rows = mine[0].shape[0]
    return pl.pallas_call(
        functools.partial(project_kernel, widths),
        in_specs=[vmem] * (1 + 2 * len(widths)),
        out_specs=vmem,
        out_shape=jax.ShapeDtypeStruct((rows, w.shape[1]), jnp.bfloat16),
        compiler_params=pltpu.CompilerParams(vmem_limit_bytes=40 << 20),
        cost_estimate=pl.CostEstimate(
            flops=2 * rows * w.shape[0] * w.shape[1], bytes_accessed=3 << 20, transcendentals=0
        ),
        name="project",
    )(w, *mine, *other)


def broadcast(parts, root_code, my_code, n):
    dims = log2_of(n)
    for r in range(dims):
        bits = [(p + r) % dims for p in range(len(parts))]
        got = [swap(x, "blk", n, b) for x, b in zip(parts, bits)]
        parts = [
            jnp.where(((root_code ^ my_code) >> b) & 1 == 1, y, x)
            for x, y, b in zip(parts, got, bits)
        ]
    return parts


def per_device(
    n_blk,
    n_head,
    ctx_q,
    ctx_k,
    ctx_v,
    query_q,
    query_k,
    query_v,
    out_weight,
    anchor_index,
    owner_index,
    counts,
):
    rows = ctx_q.shape[0]
    heads = ctx_q.shape[1] // HD
    me = lax.axis_index("blk")
    anchor, owner = anchor_index[0], owner_index[0]
    dims = log2_of(n_blk)
    my_code = code_of(me)

    q_spans = spans(heads, dims, 1)
    q_parts = [query_q[0][:, a * HD : b * HD] for a, b in q_spans]
    q_parts = broadcast(q_parts, code_of(owner), my_code, n_blk)

    bounds = spans(rows, dims, 128)
    both = jnp.concatenate([ctx_k, ctx_v], axis=1)
    kv_parts = broadcast([both[a:b] for a, b in bounds], code_of(anchor), my_code, n_blk)

    half = heads // 2
    own = [own_call(ctx_q, ctx_k, ctx_v, a, a + half) for a in (0, half)]

    q_limits = jnp.stack([counts[me], (me == owner).astype(jnp.int32)])
    parts = [
        query_call(q_limits, x, ctx_k, ctx_v, query_k, query_v, a, b)
        for x, (a, b) in zip(q_parts, q_spans)
    ]
    widths = [b - a for a, b in q_spans]
    for r in range(dims):
        other = [swap(x, "blk", n_blk, (p + r) % dims) for p, x in enumerate(parts)]
        if r < dims - 1:
            parts = merge_call(parts, other, widths)
    partial = project_call(parts, other, widths, out_weight)

    hid = lax.axis_index("head")
    top = partial.shape[0] // 2
    low, high = partial[:top], partial[top:]
    odd = (hid & 1) == 1
    keep, give = jnp.where(odd, high, low), jnp.where(odd, low, high)
    f32 = jnp.float32

    def hop(x, bit):
        return lax.ppermute(x, "head", [(i, i ^ (1 << bit)) for i in range(n_head)])

    total = keep.astype(f32) + hop(give, 0).astype(f32)
    for bit in range(1, log2_of(n_head)):
        sent = total.astype(jnp.bfloat16)
        total = sent.astype(f32) + hop(sent, bit).astype(f32)
    mine = total.astype(jnp.bfloat16)
    theirs = hop(mine, 0)
    answer = jnp.where(
        odd, jnp.concatenate([theirs, mine], axis=0), jnp.concatenate([mine, theirs], axis=0)
    )

    limits = jnp.stack([jnp.where(me == anchor, 0, counts[anchor]), counts[me]])
    out = None
    for i, a in enumerate((0, half)):
        out = anchor_call(limits, ctx_q, kv_parts, bounds, own[i], out, a, a + half)
    return out, answer


def solution(mesh):
    placed = (
        P("blk", "head"),
        P("blk", "head"),
        P("blk", "head"),
        P("blk", None, "head"),
        P("blk", None, "head"),
        P("blk", None, "head"),
        P("head", "blk"),
        P(),
        P(),
        P(),
    )
    return jax.shard_map(
        functools.partial(per_device, mesh.shape["blk"], mesh.shape["head"]),
        mesh=mesh,
        in_specs=placed,
        out_specs=(P("blk", "head"), P(None, "blk")),
        check_vma=False,
    )
```

```python
import functools
import math

import jax
import jax.numpy as jnp
from jax import lax
from jax.experimental import pallas as pl
from jax.experimental.pallas import tpu as pltpu
from jax.sharding import PartitionSpec as P


HEADS = 32
KV_HEADS = 8
GROUP = HEADS // KV_HEADS
HD = 128
C = HD**-0.5 * math.log2(math.e)
NEG = -1e30
NT = (((1,), (1,)), ((), ()))
TM = 256
VMEM = 14 << 20
WIDE = 61 << 20


def code_of(i):
    u = i >> 1
    return (i & 1) | ((u ^ (u >> 1)) << 1)


def decode_table(n):
    return {code_of(i): i for i in range(n)}


def log2_of(n):
    k = n.bit_length() - 1
    assert 1 << k == n
    return k


class Grid:
    def __init__(self, n_blk, n_head):
        self.n_blk, self.n_head = n_blk, n_head
        self.dims = log2_of(n_blk)

    def order(self, head):
        dims = list(range(self.dims))
        return dims if head & 1 == 0 else dims[1:] + dims[:1]

    def bit(self, step, odd):
        return jnp.where(odd, self.order(1)[step], self.order(0)[step])

    def hop(self, value, steps):
        back = decode_table(self.n_blk)
        pairs = []
        for i in range(self.n_blk):
            for h in range(self.n_head):
                j = back[code_of(i) ^ (1 << self.order(h)[steps])]
                pairs.append((i * self.n_head + h, j * self.n_head + h))
        return lax.ppermute(value, ("blk", "head"), pairs)

    def head_hop(self, value, bit):
        return lax.ppermute(value, "head", [(i, i ^ (1 << bit)) for i in range(self.n_head)])


def scores(q, k):
    return lax.dot_general(q, k, NT, preferred_element_type=jnp.float32)


def lane_max(s):
    m = s[:, :128]
    for j in range(1, s.shape[1] // 128):
        m = jnp.maximum(m, s[:, j * 128 : (j + 1) * 128])
    return jnp.max(m, axis=1, keepdims=True)


def weigh(p, v):
    wide = jnp.concatenate([v, jnp.ones_like(v)], axis=1)
    both = jnp.dot(p.astype(jnp.bfloat16), wide, preferred_element_type=jnp.float32)
    return both


def attend(s_parts, v_parts):
    m = functools.reduce(jnp.maximum, [lane_max(s) for s in s_parts])
    mc = m * C
    acc = None
    for s, v in zip(s_parts, v_parts):
        both = weigh(jnp.exp2(s * C - mc), v)
        acc = both if acc is None else acc + both
    return m, acc[:, HD:], acc[:, :HD]


def causal(n, width, first_col):
    r = lax.broadcasted_iota(jnp.int32, (n, width), 0)
    c = lax.broadcasted_iota(jnp.int32, (n, width), 1) + first_col
    return c <= r


def own_kernel(q_ref, k_ref, v_ref, o_ref, stat_ref):
    rows = q_ref.shape[0]
    h = pl.program_id(0)
    lane = lax.broadcasted_iota(jnp.int32, (TM, 128), 1)
    for i in range(rows // TM):
        at = pl.ds(i * TM, TM)
        q = q_ref[at, :]
        n = i * TM
        s_parts = [jnp.where(causal(TM, TM, 0), scores(q, k_ref[at, :]), NEG)]
        v_parts = [v_ref[at, :]]
        if n:
            s_parts.append(scores(q, k_ref[:n, :]))
            v_parts.append(v_ref[:n, :])
        m, total, o = attend(s_parts, v_parts)
        o_ref[at, :] = o
        stat = jnp.where(lane == h, m, stat_ref[at, :])
        stat_ref[at, :] = jnp.where(lane == h + 64, total, stat)


def own_call(q, k, v, lo, hi):
    rows = q.shape[0]
    n = hi - lo
    f32 = jnp.float32
    return pl.pallas_call(
        own_kernel,
        grid=(n,),
        in_specs=[
            pl.BlockSpec((rows, HD), lambda h: (0, lo + h)),
            pl.BlockSpec((rows, HD), lambda h: (0, (lo + h) // GROUP)),
            pl.BlockSpec((rows, HD), lambda h: (0, (lo + h) // GROUP)),
        ],
        out_specs=[
            pl.BlockSpec((rows, HD), lambda h: (0, h)),
            pl.BlockSpec((rows, 128), lambda h: (0, 0)),
        ],
        out_shape=[
            jax.ShapeDtypeStruct((rows, n * HD), f32),
            jax.ShapeDtypeStruct((rows, 128), f32),
        ],
        compiler_params=pltpu.CompilerParams(vmem_limit_bytes=WIDE),
        cost_estimate=pl.CostEstimate(
            flops=n * rows * rows * HD * 8, bytes_accessed=n * rows * HD * 10, transcendentals=0
        ),
        name="own",
    )(q, k, v)


def pick(block, lane, h):
    return jnp.max(jnp.where(lane == h, block, NEG), axis=1, keepdims=True)


def anchor_kernel(parts, n_ref, q_ref, *refs):
    k_refs, v_refs = refs[:parts], refs[parts : 2 * parts]
    o_ref, stat_ref, _, out_ref = refs[2 * parts :]
    rows = q_ref.shape[0]
    h = pl.program_id(0)
    lane = lax.broadcasted_iota(jnp.int32, (TM, 128), 1)
    bias = [
        jnp.where(
            lax.broadcasted_iota(jnp.int32, (1, k.shape[0]), 1) + n_ref[2 + p] < n_ref[0], 0.0, NEG
        )
        for p, k in enumerate(k_refs)
    ]
    for i in range(rows // TM):
        at = pl.ds(i * TM, TM)
        q = q_ref[at, :]
        s_parts = [scores(q, k[...]) + b for k, b in zip(k_refs, bias)]
        m, total, o = attend(s_parts, [v[...] for v in v_refs])
        stat = stat_ref[at, :]
        m_own, l_own = pick(stat, lane, h), pick(stat, lane, h + 64)
        top = jnp.maximum(m, m_own)
        wa, wb = jnp.exp2((m - top) * C), jnp.exp2((m_own - top) * C)
        normed = (o * wa + o_ref[at, :] * wb) / (total * wa + l_own * wb)
        row = lax.broadcasted_iota(jnp.int32, (TM, 128), 0) + i * TM
        out_ref[at, :] = jnp.where(row < n_ref[1], normed, 0.0).astype(out_ref.dtype)


def anchor_call(limits, q, halves, own, out, lo, hi):
    rows = q.shape[0]
    n = hi - lo
    kv = halves[0].shape[1] // (2 * HD)
    part = halves[0].shape[0] // 2
    arrays = [halves[0], halves[0], halves[1], halves[1]]
    k_specs = [pl.BlockSpec((part, HD), lambda h, _, p=p: (p % 2, (lo + h) // GROUP)) for p in range(4)]
    v_specs = [
        pl.BlockSpec((part, HD), lambda h, _, p=p: (p % 2, kv + (lo + h) // GROUP)) for p in range(4)
    ]
    in_specs = [
        pl.BlockSpec((rows, HD), lambda h, _: (0, lo + h)),
        *k_specs,
        *v_specs,
        pl.BlockSpec((rows, HD), lambda h, _: (0, h)),
        pl.BlockSpec((rows, 128), lambda h, _: (0, 0)),
        pl.BlockSpec(memory_space=pl.ANY),
    ]
    operands = [limits, q, *arrays, *arrays, *own, q if out is None else out]
    return pl.pallas_call(
        functools.partial(anchor_kernel, 4),
        grid_spec=pltpu.PrefetchScalarGridSpec(
            num_scalar_prefetch=1,
            grid=(n,),
            in_specs=in_specs,
            out_specs=pl.BlockSpec((rows, HD), lambda h, _: (0, lo + h)),
        ),
        out_shape=jax.ShapeDtypeStruct(q.shape, q.dtype),
        input_output_aliases={} if out is None else {len(operands) - 1: 0},
        compiler_params=pltpu.CompilerParams(vmem_limit_bytes=WIDE),
        cost_estimate=pl.CostEstimate(
            flops=n * rows * rows * HD * 12, bytes_accessed=n * rows * HD * 10, transcendentals=0
        ),
        name="anchor",
    )(*operands)


def lanes(rows):
    return lax.broadcasted_iota(jnp.int32, (rows, 128), 1)


def pack_stat(x, heads):
    lane = lanes(x.shape[0])
    hi = x.astype(jnp.bfloat16).astype(jnp.float32)
    mid = (x - hi).astype(jnp.bfloat16).astype(jnp.float32)
    low = x - hi - mid
    out = jnp.where(lane < 2 * heads, pltpu.roll(mid, heads, 1), pltpu.roll(low, 2 * heads, 1))
    return jnp.where(lane < heads, hi, out).astype(jnp.bfloat16)


def unpack_stat(block, heads):
    x = block.astype(jnp.float32)
    return x + pltpu.roll(x, 128 - heads, 1) + pltpu.roll(x, 128 - 2 * heads, 1)


def query_kernel(heads, n_ref, qa_ref, qb_ref, k_ref, v_ref, k2_ref, v2_ref, *outs):
    rows, keys, extra = qa_ref.shape[0], k_ref.shape[0], k2_ref.shape[1]
    bias = jnp.where(lax.broadcasted_iota(jnp.int32, (1, keys), 1) < n_ref[0], 0.0, NEG)
    lane = lanes(rows)
    row = lax.broadcasted_iota(jnp.int32, (rows, extra), 0)
    col = lax.broadcasted_iota(jnp.int32, (rows, extra), 1)
    for i, q_ref in enumerate((qa_ref, qb_ref)):
        seen = (col <= row + n_ref[2 + i]) & (n_ref[1] > 0)
        tops = jnp.zeros((rows, 128), jnp.float32)
        totals = jnp.ones((rows, 128), jnp.float32)
        sent_ref = outs[2] if i == 0 else outs[3]
        for h in range(heads):
            cols = slice(h * HD, (h + 1) * HD)
            at = slice(h // GROUP * HD, (h // GROUP + 1) * HD)
            q = q_ref[:, cols]
            s_parts = [
                scores(q, k_ref[:, at]) + bias,
                jnp.where(seen, scores(q, k2_ref[0, :, at]), NEG),
            ]
            m, total, o = attend(s_parts, [v_ref[:, at], v2_ref[0, :, at]])
            o = o / total
            if i == 0:
                outs[0][:, cols] = o
            else:
                sent_ref[:, cols] = o.astype(sent_ref.dtype)
            tops = jnp.where(lane == h, m, tops)
            totals = jnp.where(lane == h, total, totals)
        lse = tops * C + jnp.log2(totals)
        if i == 0:
            outs[1][...] = lse
        else:
            sent_ref[:, heads * HD :] = pack_stat(lse, heads)


def part_shapes(rows, heads):
    return [
        jax.ShapeDtypeStruct((rows, heads * HD), jnp.float32),
        jax.ShapeDtypeStruct((rows, 128), jnp.float32),
        jax.ShapeDtypeStruct((rows, heads * HD + 128), jnp.bfloat16),
    ]


def query_call(limits, qa, qb, k, v, k2, v2):
    rows, heads = qa.shape[0], qa.shape[1] // HD
    vmem = pl.BlockSpec(memory_space=pltpu.VMEM)

    def kernel(*refs):
        query_kernel(heads, *refs[:7], refs[7], refs[8], None, refs[9])

    return pl.pallas_call(
        kernel,
        in_specs=[pl.BlockSpec(memory_space=pltpu.SMEM)] + [vmem] * 6,
        out_specs=[vmem] * 3,
        out_shape=part_shapes(rows, heads),
        compiler_params=pltpu.CompilerParams(vmem_limit_bytes=VMEM),
        cost_estimate=pl.CostEstimate(
            flops=2 * heads * rows * (k.shape[0] + rows) * HD * 8,
            bytes_accessed=2 * rows * heads * HD * 4,
            transcendentals=0,
        ),
        name="query",
    )(limits, qa, qb, k, v, k2, v2)


def weights_of(lse, other):
    top = jnp.maximum(lse, other)
    wa, wb = jnp.exp2(lse - top), jnp.exp2(other - top)
    both = wa + wb
    return wa / both, wb / both, top + jnp.log2(both)


def merged(wa, wb, o_ref, got_ref, h):
    cols = slice(h * HD, (h + 1) * HD)
    return o_ref[:, cols] * wa[:, h : h + 1] + got_ref[:, cols].astype(jnp.float32) * wb[:, h : h + 1]


def merge_kernel(heads, o_ref, lse_ref, got_ref, *outs):
    wa, wb, lse = weights_of(lse_ref[...], unpack_stat(got_ref[:, heads * HD :], heads))
    for h in range(heads):
        cols = slice(h * HD, (h + 1) * HD)
        o = merged(wa, wb, o_ref, got_ref, h)
        if len(outs) == 3:
            outs[0][:, cols] = o
        outs[-1][:, cols] = o.astype(outs[-1].dtype)
    if len(outs) == 3:
        outs[1][...] = lse
        outs[2][:, heads * HD :] = pack_stat(lse, heads)


def merge_call(o, lse, got, last):
    rows, heads = o.shape[0], o.shape[1] // HD
    vmem = pl.BlockSpec(memory_space=pltpu.VMEM)
    shapes = part_shapes(rows, heads)
    if last:
        shapes = [jax.ShapeDtypeStruct((rows, heads * HD), jnp.bfloat16)]
    return pl.pallas_call(
        functools.partial(merge_kernel, heads),
        in_specs=[vmem] * 3,
        out_specs=[vmem] * len(shapes),
        out_shape=shapes,
        compiler_params=pltpu.CompilerParams(vmem_limit_bytes=VMEM),
        cost_estimate=pl.CostEstimate(flops=1 << 20, bytes_accessed=2 << 20, transcendentals=0),
        name="merge",
    )(o, lse, got)


def project_kernel(n_ref, w_ref, mine_ref, theirs_ref, out_ref):
    rows = mine_ref.shape[0]
    for i, ref in enumerate((mine_ref, theirs_ref)):
        at = pl.ds(pl.multiple_of(n_ref[2 + i], rows), rows)
        out_ref[at, :] = jnp.dot(ref[...], w_ref[...], preferred_element_type=jnp.float32)


def project_call(limits, mine, theirs, w):
    rows = mine.shape[0]
    vmem = pl.BlockSpec(memory_space=pltpu.VMEM)
    return pl.pallas_call(
        project_kernel,
        in_specs=[pl.BlockSpec(memory_space=pltpu.SMEM)] + [vmem] * 3,
        out_specs=vmem,
        out_shape=jax.ShapeDtypeStruct((2 * rows, w.shape[1]), jnp.float32),
        compiler_params=pltpu.CompilerParams(vmem_limit_bytes=VMEM),
        cost_estimate=pl.CostEstimate(
            flops=4 * rows * w.shape[0] * w.shape[1], bytes_accessed=3 << 20, transcendentals=0
        ),
        name="project",
    )(limits, w, mine, theirs)


def per_device(
    grid,
    ctx_q,
    ctx_k,
    ctx_v,
    query_q,
    query_k,
    query_v,
    out_weight,
    anchor_index,
    owner_index,
    counts,
):
    rows = ctx_q.shape[0]
    heads = ctx_q.shape[1] // HD
    me, hid = lax.axis_index("blk"), lax.axis_index("head")
    anchor, owner = anchor_index[0], owner_index[0]
    my_code = code_of(me)
    f32 = jnp.float32

    odd = (hid & 1) == 1

    def side_of(step):
        return (my_code >> grid.bit(step, odd)) & 1

    def far(root, step):
        return ((code_of(root) ^ my_code) >> grid.bit(step, odd)) & 1 == 1

    def hop(x, step):
        return grid.hop(x, step)

    def cut(x, side):
        half = x.shape[0] // 2
        return lax.dynamic_slice_in_dim(x, side * half, half, 0)

    last = grid.dims - 1
    side = side_of(0)
    query = query_q[0]
    q_rows = query.shape[0] // 2
    qa = jnp.where(far(owner, 0), hop(cut(query, 1 - side), 0), cut(query, side))
    for step in range(1, grid.dims):
        qa = jnp.where(far(owner, step), hop(qa, step), qa)
    qb = hop(qa, 0)

    side1 = side_of(1)

    def both(cutter):
        return jnp.concatenate([cutter(ctx_k), cutter(ctx_v)], axis=1)

    mine = jnp.where(
        far(anchor, 0),
        hop(both(lambda x: cut(x, 1 - side)), 0),
        both(lambda x: cut(x, side)),
    )
    mine = jnp.where(far(anchor, 1), hop(cut(mine, 1 - side1), 1), cut(mine, side1))
    for step in range(2, grid.dims):
        mine = jnp.where(far(anchor, step), hop(mine, step), mine)
    mine = jnp.concatenate([mine, hop(mine, 1)], axis=0)
    halves = [mine, hop(mine, 0)]
    part = rows // 4
    starts = [
        2 * part * s0 + part * s1 for s0 in (side, 1 - side) for s1 in (side1, 1 - side1)
    ]

    pieces = 4
    width = heads // pieces
    cuts = [(i * width, (i + 1) * width) for i in range(pieces)]
    own = []
    for a, b in cuts:
        own.append(own_call(ctx_q, ctx_k, ctx_v, a, b))

    q_limits = jnp.stack(
        [counts[me], (me == owner).astype(jnp.int32), side * q_rows, (1 - side) * q_rows]
    )
    o, lse, sent = query_call(q_limits, qa, qb, ctx_k, ctx_v, query_k, query_v)
    for step in range(grid.dims):
        got = hop(sent, step)
        done = merge_call(o, lse, got, step == last)
        if step < last:
            o, lse, sent = done
    theirs = hop(done[0], 0)
    partial = project_call(q_limits, done[0], theirs, out_weight)

    top = partial.shape[0] // 2
    low, high = partial[:top], partial[top:]
    keep, give = jnp.where(odd, high, low), jnp.where(odd, low, high)
    got = grid.head_hop(give, 0)
    total = keep + got
    for bit in range(1, log2_of(grid.n_head)):
        sent = total.astype(jnp.bfloat16)
        got = grid.head_hop(sent, bit)
        total = sent.astype(f32) + got.astype(f32)
    ours = total.astype(jnp.bfloat16)
    rest = grid.head_hop(ours, 0)
    answer = jnp.where(
        odd, jnp.concatenate([rest, ours], axis=0), jnp.concatenate([ours, rest], axis=0)
    )

    limits = jnp.stack([jnp.where(me == anchor, 0, counts[anchor]), counts[me], *starts])
    out = None
    for i, (a, b) in enumerate(cuts):
        out = anchor_call(limits, ctx_q, halves, own[i], out, a, b)
    return out, answer


def solution(mesh):
    placed = (
        P("blk", "head"),
        P("blk", "head"),
        P("blk", "head"),
        P("blk", None, "head"),
        P("blk", None, "head"),
        P("blk", None, "head"),
        P("head", "blk"),
        P(),
        P(),
        P(),
    )
    grid = Grid(mesh.shape["blk"], mesh.shape["head"])

    def whole(*args):
        return per_device(grid, *args)

    return jax.shard_map(
        whole,
        mesh=mesh,
        in_specs=placed,
        out_specs=(P("blk", "head"), P(None, "blk")),
        check_vma=False,
    )
```

```python
import functools
import math

import jax
import jax.numpy as jnp
from jax import lax
from jax.experimental import pallas as pl
from jax.experimental.pallas import tpu as pltpu
from jax.sharding import PartitionSpec as P


HEADS = 32
KV_HEADS = 8
GROUP = HEADS // KV_HEADS
HD = 128
C = HD**-0.5 * math.log2(math.e)
NEG = -1e30
NT = (((1,), (1,)), ((), ()))
TM = 256
VMEM = 8 << 20
WIDE = 8 << 20


def code_of(i):
    u = i >> 1
    return (i & 1) | ((u ^ (u >> 1)) << 1)


def decode_table(n):
    return {code_of(i): i for i in range(n)}


def log2_of(n):
    k = n.bit_length() - 1
    assert 1 << k == n
    return k


class Grid:
    def __init__(self, n_blk, n_head):
        self.n_blk, self.n_head = n_blk, n_head
        self.dims = log2_of(n_blk)

    def order(self, head):
        dims = list(range(self.dims))
        return dims if head & 1 == 0 else dims[1:] + dims[:1]

    def bit(self, step, odd):
        return jnp.where(odd, self.order(1)[step], self.order(0)[step])

    def hop(self, value, steps):
        back = decode_table(self.n_blk)
        pairs = []
        for i in range(self.n_blk):
            for h in range(self.n_head):
                j = back[code_of(i) ^ (1 << self.order(h)[steps])]
                pairs.append((i * self.n_head + h, j * self.n_head + h))
        return lax.ppermute(value, ("blk", "head"), pairs)

    def head_hop(self, value, bit):
        return lax.ppermute(value, "head", [(i, i ^ (1 << bit)) for i in range(self.n_head)])


def scores(q, k):
    return lax.dot_general(q, k, NT, preferred_element_type=jnp.float32) * C


def top_of(s_parts):
    m = None
    for s in s_parts:
        for j in range(s.shape[1] // 128):
            x = s[:, j * 128 : (j + 1) * 128]
            m = x if m is None else jnp.maximum(m, x)
    return jnp.max(m, axis=1, keepdims=True)


def wide(v):
    return jnp.concatenate([v, jnp.ones_like(v)], axis=1)


def attend(s_parts, wide_parts):
    m = top_of(s_parts)
    acc = None
    for s, v in zip(s_parts, wide_parts):
        p = jnp.exp2(s - m).astype(jnp.bfloat16)
        both = jnp.dot(p, v, preferred_element_type=jnp.float32)
        acc = both if acc is None else acc + both
    return m, acc[:, HD:], acc[:, :HD]


def causal(n, width, first_col):
    r = lax.broadcasted_iota(jnp.int32, (n, width), 0)
    c = lax.broadcasted_iota(jnp.int32, (n, width), 1) + first_col
    return c <= r


def own_kernel(lo, q_ref, k_ref, v_ref, *refs):
    o_ref, stat_ref = refs[-2:]
    rows = q_ref.shape[0]
    h = pl.program_id(0)
    lane = lanes(TM)

    if len(refs) == 4:

        @pl.when(h == 0)
        def _():
            stat_ref[...] = refs[1][...]

    def score(i):
        q = q_ref[i * TM : (i + 1) * TM, :]
        parts = [scores(q, k_ref[j * TM : (j + 1) * TM, :]) for j in range(i)]
        diagonal = scores(q, k_ref[i * TM : (i + 1) * TM, :])
        return parts + [jnp.where(causal(TM, TM, 0), diagonal, NEG)]

    ready = score(0)
    for i in range(rows // TM):
        at = pl.ds(i * TM, TM)
        s_parts = ready
        if (i + 1) * TM < rows:
            ready = score(i + 1)
        m, total, o = attend(s_parts, [wide(v_ref[j * TM : (j + 1) * TM, :]) for j in range(i + 1)])
        o_ref[at, :] = o
        put_stat(stat_ref, at, lane, lo + h, m, total)


def put_stat(ref, at, lane, h, m, total):
    stat = jnp.where(lane == h, m, ref[at, :])
    ref[at, :] = jnp.where(lane == h + 64, total, stat)


def state_shapes(q):
    return [
        jax.ShapeDtypeStruct(q.shape, jnp.float32),
        jax.ShapeDtypeStruct((q.shape[0], 128), jnp.float32),
    ]


def own_call(q, k, v, state, lo, hi):
    rows = q.shape[0]
    n = hi - lo
    head = pl.BlockSpec((rows, HD), lambda h: (0, lo + h))
    stat = pl.BlockSpec((rows, 128), lambda h: (0, 0))
    group = pl.BlockSpec((rows, HD), lambda h: (0, (lo + h) // GROUP))
    more = [] if state is None else [pl.BlockSpec(memory_space=pl.ANY), stat]
    return pl.pallas_call(
        functools.partial(own_kernel, lo),
        grid=(n,),
        in_specs=[head, group, group, *more],
        out_specs=[head, stat],
        out_shape=state_shapes(q),
        input_output_aliases={} if state is None else {3: 0, 4: 1},
        compiler_params=pltpu.CompilerParams(vmem_limit_bytes=WIDE),
        cost_estimate=pl.CostEstimate(
            flops=n * rows * rows * HD * 8, bytes_accessed=n * rows * HD * 10, transcendentals=0
        ),
        name="own",
    )(q, k, v, *([] if state is None else state))


def pick(block, lane, h):
    return jnp.max(jnp.where(lane == h, block, NEG), axis=1, keepdims=True)


def anchor_kernel(lo, parts, seen_at, final, n_ref, q_ref, *refs):
    k_refs, v_refs = refs[:parts], refs[parts : 2 * parts]
    o_ref, stat_ref = refs[2 * parts : 2 * parts + 2]
    k_all, v_all = refs[-2:]
    outs = refs[2 * parts + (3 if final else 2) : -2]
    rows, part = q_ref.shape[0], k_refs[0].shape[0]
    h = pl.program_id(0)
    lane = lanes(TM)
    seen = n_ref[seen_at]

    @pl.when((h == 0) | ((lo + h) % GROUP == 0))
    def _():
        for p in range(parts):
            at = pl.ds(pl.multiple_of(n_ref[seen_at + 1 + p], part), part)
            k_all[at, :] = k_refs[p][...]
            v_all[at, :] = wide(v_refs[p][...])

    if not final:

        @pl.when(h == 0)
        def _():
            outs[1][...] = stat_ref[...]

    def store(i, m, total, o):
        at = pl.ds(i * TM, TM)
        stat = stat_ref[at, :]
        m_own, l_own = pick(stat, lane, lo + h), pick(stat, lane, lo + h + 64)
        top = jnp.maximum(m, m_own)
        wa, wb = jnp.exp2(m - top), jnp.exp2(m_own - top)
        both, l_both = o * wa + o_ref[at, :] * wb, total * wa + l_own * wb
        if final:
            finish(i, both, l_both)
        else:
            outs[0][at, :] = both
            put_stat(outs[1], at, lane, lo + h, top, l_both)

    def finish(i, o, total):
        row = lax.broadcasted_iota(jnp.int32, (TM, 128), 0) + i * TM
        normed = jnp.where(row < n_ref[0], o / total, 0.0)
        outs[0][pl.ds(i * TM, TM), :] = normed.astype(outs[0].dtype)

    @pl.when(seen <= 0)
    def _():
        for i in range(rows // TM):
            at = pl.ds(i * TM, TM)
            if final:
                finish(i, o_ref[at, :], pick(stat_ref[at, :], lane, lo + h + 64))
            else:
                outs[0][at, :] = o_ref[at, :]

    for n in range(1, parts + 1):
        low = seen > (n - 1) * part

        @pl.when(low & (seen <= n * part) if n < parts else low)
        def _(n=n):
            col = lax.broadcasted_iota(jnp.int32, (1, part), 1) + (n - 1) * part
            bias = jnp.where(col < seen, 0.0, NEG)

            def score(i):
                q = q_ref[i * TM : (i + 1) * TM, :]
                parts = [scores(q, k_all[j * part : (j + 1) * part, :]) for j in range(n)]
                return parts[:-1] + [parts[-1] + bias]

            ready = score(0)
            for i in range(rows // TM):
                s_parts = ready
                if (i + 1) * TM < rows:
                    ready = score(i + 1)
                store(i, *attend(s_parts, [v_all[j * part : (j + 1) * part, :] for j in range(n)]))


def anchor_call(table, seen_at, q, kv, state, lo, hi, final=False, out=None):
    rows = q.shape[0]
    n, parts = hi - lo, 2 * len(kv)
    base = kv[0].shape[1] // (2 * HD)
    part = kv[0].shape[0] // 2
    head = pl.BlockSpec((rows, HD), lambda h, _: (0, lo + h))
    stat = pl.BlockSpec((rows, 128), lambda h, _: (0, 0))

    def block(p, at):
        return pl.BlockSpec((part, HD), lambda h, _: (p % 2, at + (lo + h) // GROUP))

    in_specs = [head]
    in_specs += [block(p, 0) for p in range(parts)] + [block(p, base) for p in range(parts)]
    in_specs += [head, stat]
    operands = [table, q] + [kv[p // 2] for p in range(parts)] * 2 + list(state)
    if final:
        in_specs.append(pl.BlockSpec(memory_space=pl.ANY))
        operands.append(q if out is None else out)
        shapes, out_specs = [jax.ShapeDtypeStruct(q.shape, q.dtype)], [head]
        aliases = {} if out is None else {len(operands) - 1: 0}
    else:
        shapes, out_specs = state_shapes(q), [head, stat]
        aliases = {len(operands) - 2: 0, len(operands) - 1: 1}
    return pl.pallas_call(
        functools.partial(anchor_kernel, lo, parts, seen_at, final),
        grid_spec=pltpu.PrefetchScalarGridSpec(
            num_scalar_prefetch=1,
            grid=(n,),
            in_specs=in_specs,
            out_specs=out_specs,
            scratch_shapes=[
                pltpu.VMEM((parts * part, HD), q.dtype),
                pltpu.VMEM((parts * part, 2 * HD), q.dtype),
            ],
        ),
        out_shape=shapes,
        input_output_aliases=aliases,
        compiler_params=pltpu.CompilerParams(vmem_limit_bytes=WIDE),
        cost_estimate=pl.CostEstimate(
            flops=n * rows * rows * HD * 3 * parts,
            bytes_accessed=n * rows * HD * 10,
            transcendentals=0,
        ),
        name="anchor",
    )(*operands)


def lanes(rows):
    return lax.broadcasted_iota(jnp.int32, (rows, 128), 1)


def pack_stat(x, heads):
    lane = lanes(x.shape[0])
    hi = x.astype(jnp.bfloat16).astype(jnp.float32)
    mid = (x - hi).astype(jnp.bfloat16).astype(jnp.float32)
    low = x - hi - mid
    out = jnp.where(lane < 2 * heads, pltpu.roll(mid, heads, 1), pltpu.roll(low, 2 * heads, 1))
    return jnp.where(lane < heads, hi, out).astype(jnp.bfloat16)


def unpack_stat(block, heads):
    x = block.astype(jnp.float32)
    return x + pltpu.roll(x, 128 - heads, 1) + pltpu.roll(x, 128 - 2 * heads, 1)


def query_kernel(heads, n_ref, qa_ref, qb_ref, k_ref, v_ref, k2_ref, v2_ref, *outs):
    rows, keys, extra = qa_ref.shape[0], k_ref.shape[0], k2_ref.shape[1]
    bias = jnp.where(lax.broadcasted_iota(jnp.int32, (1, keys), 1) < n_ref[0], 0.0, NEG)
    lane = lanes(rows)
    row = lax.broadcasted_iota(jnp.int32, (rows, extra), 0)
    col = lax.broadcasted_iota(jnp.int32, (rows, extra), 1)
    for i, q_ref in enumerate((qa_ref, qb_ref)):
        seen = (col <= row + n_ref[2 + i]) & (n_ref[1] > 0)
        tops = jnp.zeros((rows, 128), jnp.float32)
        totals = jnp.ones((rows, 128), jnp.float32)
        sent_ref = outs[2] if i == 0 else outs[3]
        for h in range(heads):
            cols = slice(h * HD, (h + 1) * HD)
            at = slice(h // GROUP * HD, (h // GROUP + 1) * HD)
            q = q_ref[:, cols]
            s_parts = [
                scores(q, k_ref[:, at]) + bias,
                jnp.where(seen, scores(q, k2_ref[0, :, at]), NEG),
            ]
            m, total, o = attend(s_parts, [wide(v_ref[:, at]), wide(v2_ref[0, :, at])])
            o = o / total
            if i == 0:
                outs[0][:, cols] = o
            else:
                sent_ref[:, cols] = o.astype(sent_ref.dtype)
            tops = jnp.where(lane == h, m, tops)
            totals = jnp.where(lane == h, total, totals)
        lse = tops + jnp.log2(totals)
        if i == 0:
            outs[1][...] = lse
        else:
            sent_ref[:, heads * HD :] = pack_stat(lse, heads)


def part_shapes(rows, heads):
    return [
        jax.ShapeDtypeStruct((rows, heads * HD), jnp.float32),
        jax.ShapeDtypeStruct((rows, 128), jnp.float32),
        jax.ShapeDtypeStruct((rows, heads * HD + 128), jnp.bfloat16),
    ]


def query_call(limits, qa, qb, k, v, k2, v2):
    rows, heads = qa.shape[0], qa.shape[1] // HD
    vmem = pl.BlockSpec(memory_space=pltpu.VMEM)

    def kernel(*refs):
        query_kernel(heads, *refs[:7], refs[7], refs[8], None, refs[9])

    return pl.pallas_call(
        kernel,
        in_specs=[pl.BlockSpec(memory_space=pltpu.SMEM)] + [vmem] * 6,
        out_specs=[vmem] * 3,
        out_shape=part_shapes(rows, heads),
        compiler_params=pltpu.CompilerParams(vmem_limit_bytes=VMEM),
        cost_estimate=pl.CostEstimate(
            flops=2 * heads * rows * (k.shape[0] + rows) * HD * 8,
            bytes_accessed=2 * rows * heads * HD * 4,
            transcendentals=0,
        ),
        name="query",
    )(limits, qa, qb, k, v, k2, v2)


def weights_of(lse, other):
    top = jnp.maximum(lse, other)
    wa, wb = jnp.exp2(lse - top), jnp.exp2(other - top)
    both = wa + wb
    return wa / both, wb / both, top + jnp.log2(both)


def merged(wa, wb, o_ref, got_ref, h):
    cols = slice(h * HD, (h + 1) * HD)
    return o_ref[:, cols] * wa[:, h : h + 1] + got_ref[:, cols].astype(jnp.float32) * wb[:, h : h + 1]


def merge_kernel(heads, o_ref, lse_ref, got_ref, *outs):
    wa, wb, lse = weights_of(lse_ref[...], unpack_stat(got_ref[:, heads * HD :], heads))
    for h in range(heads):
        cols = slice(h * HD, (h + 1) * HD)
        o = merged(wa, wb, o_ref, got_ref, h)
        if len(outs) == 3:
            outs[0][:, cols] = o
        outs[-1][:, cols] = o.astype(outs[-1].dtype)
    if len(outs) == 3:
        outs[1][...] = lse
        outs[2][:, heads * HD :] = pack_stat(lse, heads)


def merge_call(o, lse, got, last):
    rows, heads = o.shape[0], o.shape[1] // HD
    vmem = pl.BlockSpec(memory_space=pltpu.VMEM)
    shapes = part_shapes(rows, heads)
    if last:
        shapes = [jax.ShapeDtypeStruct((rows, heads * HD), jnp.bfloat16)]
    return pl.pallas_call(
        functools.partial(merge_kernel, heads),
        in_specs=[vmem] * 3,
        out_specs=[vmem] * len(shapes),
        out_shape=shapes,
        compiler_params=pltpu.CompilerParams(vmem_limit_bytes=VMEM),
        cost_estimate=pl.CostEstimate(flops=1 << 20, bytes_accessed=2 << 20, transcendentals=0),
        name="merge",
    )(o, lse, got)


def project_kernel(n_ref, w_ref, mine_ref, theirs_ref, out_ref):
    rows = mine_ref.shape[0]
    for i, ref in enumerate((mine_ref, theirs_ref)):
        at = pl.ds(pl.multiple_of(n_ref[2 + i], rows), rows)
        out_ref[at, :] = jnp.dot(ref[...], w_ref[...], preferred_element_type=jnp.float32)


def project_call(limits, mine, theirs, w):
    rows = mine.shape[0]
    vmem = pl.BlockSpec(memory_space=pltpu.VMEM)
    return pl.pallas_call(
        project_kernel,
        in_specs=[pl.BlockSpec(memory_space=pltpu.SMEM)] + [vmem] * 3,
        out_specs=vmem,
        out_shape=jax.ShapeDtypeStruct((2 * rows, w.shape[1]), jnp.float32),
        compiler_params=pltpu.CompilerParams(vmem_limit_bytes=VMEM),
        cost_estimate=pl.CostEstimate(
            flops=4 * rows * w.shape[0] * w.shape[1], bytes_accessed=3 << 20, transcendentals=0
        ),
        name="project",
    )(limits, w, mine, theirs)


def runs(total, shares):
    whole, at, out = sum(shares), 0, []
    for i in range(len(shares)):
        end = total * sum(shares[: i + 1]) // whole
        out.append((at, end))
        at = end
    return out


def per_device(
    grid,
    ctx_q,
    ctx_k,
    ctx_v,
    query_q,
    query_k,
    query_v,
    out_weight,
    anchor_index,
    owner_index,
    counts,
):
    rows = ctx_q.shape[0]
    heads = ctx_q.shape[1] // HD
    me, hid = lax.axis_index("blk"), lax.axis_index("head")
    anchor, owner = anchor_index[0], owner_index[0]
    my_code = code_of(me)
    f32 = jnp.float32

    odd = (hid & 1) == 1

    def side_of(step):
        return (my_code >> grid.bit(step, odd)) & 1

    def is_far(root, step):
        return ((code_of(root) ^ my_code) >> grid.bit(step, odd)) & 1 == 1

    def hop(x, step):
        return grid.hop(x, step)

    def cut(x, first):
        sizes = (x.shape[0] // 2, x.shape[1])
        zero = jnp.zeros((), first.dtype)
        return lax.dynamic_slice(x, (first, zero), sizes, allow_negative_indices=False)

    side, side1 = side_of(0), side_of(1)
    query = query_q[0]
    got = hop(cut(query, (1 - side) * (query.shape[0] // 2)), 0)

    q_rows, part = query.shape[0] // 2, rows // 4
    places = [part * side1, part * (1 - side1)]
    in_view = jnp.where(me == anchor, 0, counts[anchor])
    table = jnp.stack(
        [
            counts[me],
            (me == owner).astype(jnp.int32),
            side * q_rows,
            (1 - side) * q_rows,
            in_view - 2 * part * side,
            *places,
            in_view - 2 * part * (1 - side),
            *places,
            in_view,
            *[2 * part * s0 + x for s0 in (side, 1 - side) for x in places],
        ]
    )
    q_far = [is_far(owner, step) for step in range(grid.dims)]
    a_far = [is_far(anchor, step) for step in range(grid.dims)]
    half = rows // 2
    firsts = [side * q_rows, side * half, (1 - side) * half, side1 * part, (1 - side1) * part]
    firsts, table, q_far, a_far, odd, query, ctx_q, ctx_k, ctx_v = lax.optimization_barrier(
        (firsts, table, q_far, a_far, odd, query, ctx_q, ctx_k, ctx_v)
    )

    last = grid.dims - 1
    qa = jnp.where(q_far[0], got, cut(query, firsts[0]))
    for step in range(1, grid.dims):
        qa = jnp.where(q_far[step], hop(qa, step), qa)
    qb = hop(qa, 0)

    def both(cutter):
        return jnp.concatenate([cutter(ctx_k), cutter(ctx_v)], axis=1)

    mine = jnp.where(
        a_far[0],
        hop(both(lambda x: cut(x, firsts[2])), 0),
        both(lambda x: cut(x, firsts[1])),
    )
    mine = jnp.where(a_far[1], hop(cut(mine, firsts[4]), 1), cut(mine, firsts[3]))
    for step in range(2, grid.dims):
        mine = jnp.where(a_far[step], hop(mine, step), mine)
    mine = jnp.concatenate([mine, hop(mine, 1)], axis=0)
    halves = [mine, hop(mine, 0)]

    state = None
    for a, b in runs(heads, (2, 2, 2, 2)):
        state = own_call(ctx_q, ctx_k, ctx_v, state, a, b)

    o, lse, sent = query_call(table, qa, qb, ctx_k, ctx_v, query_k, query_v)
    for step in range(grid.dims):
        got = hop(sent, step)
        done = merge_call(o, lse, got, step == last)
        if step < last:
            o, lse, sent = done
    theirs = hop(done[0], 0)
    partial = project_call(table, done[0], theirs, out_weight)

    top = partial.shape[0] // 2
    low, high = partial[:top], partial[top:]
    keep, give = jnp.where(odd, high, low), jnp.where(odd, low, high)
    got = grid.head_hop(give, 0)
    total = keep + got
    for bit in range(1, log2_of(grid.n_head)):
        sent = total.astype(jnp.bfloat16)
        got = grid.head_hop(sent, bit)
        total = sent.astype(f32) + got.astype(f32)
    ours = total.astype(jnp.bfloat16)
    rest = grid.head_hop(ours, 0)
    answer = jnp.where(
        odd, jnp.concatenate([rest, ours], axis=0), jnp.concatenate([ours, rest], axis=0)
    )

    cuts = runs(heads, (2, 2, 2, 2))
    state = anchor_call(table, 4, ctx_q, halves[:1], state, *cuts[0])
    out = None
    for a, b in cuts[1:]:
        (out,) = anchor_call(table, 10, ctx_q, halves, state, a, b, final=True, out=out)
    (out,) = anchor_call(
        table, 7, ctx_q, halves[1:], state, *cuts[0], final=True, out=out
    )
    return out, answer


def solution(mesh):
    placed = (
        P("blk", "head"),
        P("blk", "head"),
        P("blk", "head"),
        P("blk", None, "head"),
        P("blk", None, "head"),
        P("blk", None, "head"),
        P("head", "blk"),
        P(),
        P(),
        P(),
    )
    grid = Grid(mesh.shape["blk"], mesh.shape["head"])

    def whole(*args):
        return per_device(grid, *args)

    return jax.shard_map(
        whole,
        mesh=mesh,
        in_specs=placed,
        out_specs=(P("blk", "head"), P(None, "blk")),
        check_vma=False,
    )
```

```python
import functools
import math

import jax
import jax.numpy as jnp
from jax import lax
from jax.experimental import pallas as pl
from jax.experimental.pallas import tpu as pltpu
from jax.sharding import PartitionSpec as P


HEADS = 32
KV_HEADS = 8
GROUP = HEADS // KV_HEADS
HD = 128
C = HD**-0.5 * math.log2(math.e)
NEG = -1e30
NT = (((1,), (1,)), ((), ()))
TM = 256
VMEM = 8 << 20
WIDE = 8 << 20


def code_of(i):
    u = i >> 1
    return (i & 1) | ((u ^ (u >> 1)) << 1)


def decode_table(n):
    return {code_of(i): i for i in range(n)}


def log2_of(n):
    k = n.bit_length() - 1
    assert 1 << k == n
    return k


class Grid:
    def __init__(self, n_blk, n_head):
        self.n_blk, self.n_head = n_blk, n_head
        self.dims = log2_of(n_blk)

    def order(self, head):
        dims = list(range(self.dims))
        return dims if head & 1 == 0 else dims[1:] + dims[:1]

    def bit(self, step, odd):
        return jnp.where(odd, self.order(1)[step], self.order(0)[step])

    def hop(self, value, steps):
        back = decode_table(self.n_blk)
        pairs = []
        for i in range(self.n_blk):
            for h in range(self.n_head):
                j = back[code_of(i) ^ (1 << self.order(h)[steps])]
                pairs.append((i * self.n_head + h, j * self.n_head + h))
        return lax.ppermute(value, ("blk", "head"), pairs)

    def head_hop(self, value, bit):
        return lax.ppermute(value, "head", [(i, i ^ (1 << bit)) for i in range(self.n_head)])


def scores(q, k):
    return lax.dot_general(q, k, NT, preferred_element_type=jnp.float32) * C


def top_of(s_parts):
    m = None
    for s in s_parts:
        for j in range(s.shape[1] // 128):
            x = s[:, j * 128 : (j + 1) * 128]
            m = x if m is None else jnp.maximum(m, x)
    return jnp.max(m, axis=1, keepdims=True)


def wide(v):
    return jnp.concatenate([v, jnp.ones_like(v)], axis=1)


def attend(s_parts, wide_parts):
    m = top_of(s_parts)
    acc = None
    for s, v in zip(s_parts, wide_parts):
        p = jnp.exp2(s - m).astype(jnp.bfloat16)
        both = jnp.dot(p, v, preferred_element_type=jnp.float32)
        acc = both if acc is None else acc + both
    return m, acc[:, HD:], acc[:, :HD]


def causal(n, width, first_col):
    r = lax.broadcasted_iota(jnp.int32, (n, width), 0)
    c = lax.broadcasted_iota(jnp.int32, (n, width), 1) + first_col
    return c <= r


def own_kernel(lo, q_ref, k_ref, v_ref, *refs):
    o_ref, stat_ref = refs[-2:]
    rows = q_ref.shape[0]
    h = pl.program_id(0)
    lane = lanes(TM)

    if len(refs) == 4:

        @pl.when(h == 0)
        def _():
            stat_ref[...] = refs[1][...]

    def score(i):
        q = q_ref[i * TM : (i + 1) * TM, :]
        parts = [scores(q, k_ref[j * TM : (j + 1) * TM, :]) for j in range(i)]
        diagonal = scores(q, k_ref[i * TM : (i + 1) * TM, :])
        return parts + [jnp.where(causal(TM, TM, 0), diagonal, NEG)]

    ready = score(0)
    for i in range(rows // TM):
        at = pl.ds(i * TM, TM)
        s_parts = ready
        if (i + 1) * TM < rows:
            ready = score(i + 1)
        m, total, o = attend(s_parts, [wide(v_ref[j * TM : (j + 1) * TM, :]) for j in range(i + 1)])
        o_ref[at, :] = o
        put_stat(stat_ref, at, lane, lo + h, m, total)


def put_stat(ref, at, lane, h, m, total):
    stat = jnp.where(lane == h, m, ref[at, :])
    ref[at, :] = jnp.where(lane == h + 64, total, stat)


def state_shapes(q):
    return [
        jax.ShapeDtypeStruct(q.shape, jnp.float32),
        jax.ShapeDtypeStruct((q.shape[0], 128), jnp.float32),
    ]


def own_call(q, k, v, state, lo, hi):
    rows = q.shape[0]
    n = hi - lo
    head = pl.BlockSpec((rows, HD), lambda h: (0, lo + h))
    stat = pl.BlockSpec((rows, 128), lambda h: (0, 0))
    group = pl.BlockSpec((rows, HD), lambda h: (0, (lo + h) // GROUP))
    more = [] if state is None else [pl.BlockSpec(memory_space=pl.ANY), stat]
    return pl.pallas_call(
        functools.partial(own_kernel, lo),
        grid=(n,),
        in_specs=[head, group, group, *more],
        out_specs=[head, stat],
        out_shape=state_shapes(q),
        input_output_aliases={} if state is None else {3: 0, 4: 1},
        compiler_params=pltpu.CompilerParams(vmem_limit_bytes=WIDE),
        cost_estimate=pl.CostEstimate(
            flops=n * rows * rows * HD * 8, bytes_accessed=n * rows * HD * 10, transcendentals=0
        ),
        name="own",
    )(q, k, v, *([] if state is None else state))


def pick(block, lane, h):
    return jnp.max(jnp.where(lane == h, block, NEG), axis=1, keepdims=True)


def anchor_kernel(lo, parts, seen_at, final, n_ref, q_ref, *refs):
    k_refs, v_refs = refs[:parts], refs[parts : 2 * parts]
    o_ref, stat_ref = refs[2 * parts : 2 * parts + 2]
    k_all, v_all = refs[-2:]
    outs = refs[2 * parts + (3 if final else 2) : -2]
    rows, part = q_ref.shape[0], k_refs[0].shape[0]
    h = pl.program_id(0)
    lane = lanes(TM)
    seen = n_ref[seen_at]

    @pl.when((h == 0) | ((lo + h) % GROUP == 0))
    def _():
        for p in range(parts):
            at = pl.ds(pl.multiple_of(n_ref[seen_at + 1 + p], part), part)
            k_all[at, :] = k_refs[p][...]
            v_all[at, :] = wide(v_refs[p][...])

    if not final:

        @pl.when(h == 0)
        def _():
            outs[1][...] = stat_ref[...]

    def store(i, m, total, o):
        at = pl.ds(i * TM, TM)
        stat = stat_ref[at, :]
        m_own, l_own = pick(stat, lane, lo + h), pick(stat, lane, lo + h + 64)
        top = jnp.maximum(m, m_own)
        wa, wb = jnp.exp2(m - top), jnp.exp2(m_own - top)
        both, l_both = o * wa + o_ref[at, :] * wb, total * wa + l_own * wb
        if final:
            finish(i, both, l_both)
        else:
            outs[0][at, :] = both
            put_stat(outs[1], at, lane, lo + h, top, l_both)

    def finish(i, o, total):
        row = lax.broadcasted_iota(jnp.int32, (TM, 128), 0) + i * TM
        normed = jnp.where(row < n_ref[0], o / total, 0.0)
        outs[0][pl.ds(i * TM, TM), :] = normed.astype(outs[0].dtype)

    @pl.when(seen <= 0)
    def _():
        for i in range(rows // TM):
            at = pl.ds(i * TM, TM)
            if final:
                finish(i, o_ref[at, :], pick(stat_ref[at, :], lane, lo + h + 64))
            else:
                outs[0][at, :] = o_ref[at, :]

    for n in range(1, parts + 1):
        low = seen > (n - 1) * part

        @pl.when(low & (seen <= n * part) if n < parts else low)
        def _(n=n):
            col = lax.broadcasted_iota(jnp.int32, (1, part), 1) + (n - 1) * part
            bias = jnp.where(col < seen, 0.0, NEG)

            def score(i):
                q = q_ref[i * TM : (i + 1) * TM, :]
                parts = [scores(q, k_all[j * part : (j + 1) * part, :]) for j in range(n)]
                return parts[:-1] + [parts[-1] + bias]

            ready = score(0)
            for i in range(rows // TM):
                s_parts = ready
                if (i + 1) * TM < rows:
                    ready = score(i + 1)
                store(i, *attend(s_parts, [v_all[j * part : (j + 1) * part, :] for j in range(n)]))


def anchor_call(table, seen_at, q, kv, state, lo, hi, final=False, out=None):
    rows = q.shape[0]
    n, parts = hi - lo, 2 * len(kv)
    base = kv[0].shape[1] // (2 * HD)
    part = kv[0].shape[0] // 2
    head = pl.BlockSpec((rows, HD), lambda h, _: (0, lo + h))
    stat = pl.BlockSpec((rows, 128), lambda h, _: (0, 0))

    def block(p, at):
        return pl.BlockSpec((part, HD), lambda h, _: (p % 2, at + (lo + h) // GROUP))

    in_specs = [head]
    in_specs += [block(p, 0) for p in range(parts)] + [block(p, base) for p in range(parts)]
    in_specs += [head, stat]
    operands = [table, q] + [kv[p // 2] for p in range(parts)] * 2 + list(state)
    if final:
        in_specs.append(pl.BlockSpec(memory_space=pl.ANY))
        operands.append(q if out is None else out)
        shapes, out_specs = [jax.ShapeDtypeStruct(q.shape, q.dtype)], [head]
        aliases = {} if out is None else {len(operands) - 1: 0}
    else:
        shapes, out_specs = state_shapes(q), [head, stat]
        aliases = {len(operands) - 2: 0, len(operands) - 1: 1}
    return pl.pallas_call(
        functools.partial(anchor_kernel, lo, parts, seen_at, final),
        grid_spec=pltpu.PrefetchScalarGridSpec(
            num_scalar_prefetch=1,
            grid=(n,),
            in_specs=in_specs,
            out_specs=out_specs,
            scratch_shapes=[
                pltpu.VMEM((parts * part, HD), q.dtype),
                pltpu.VMEM((parts * part, 2 * HD), q.dtype),
            ],
        ),
        out_shape=shapes,
        input_output_aliases=aliases,
        compiler_params=pltpu.CompilerParams(vmem_limit_bytes=WIDE),
        cost_estimate=pl.CostEstimate(
            flops=n * rows * rows * HD * 3 * parts,
            bytes_accessed=n * rows * HD * 10,
            transcendentals=0,
        ),
        name="anchor",
    )(*operands)


def lanes(rows):
    return lax.broadcasted_iota(jnp.int32, (rows, 128), 1)


def pack_stat(x, heads):
    lane = lanes(x.shape[0])
    hi = x.astype(jnp.bfloat16).astype(jnp.float32)
    mid = (x - hi).astype(jnp.bfloat16).astype(jnp.float32)
    low = x - hi - mid
    out = jnp.where(lane < 2 * heads, pltpu.roll(mid, heads, 1), pltpu.roll(low, 2 * heads, 1))
    return jnp.where(lane < heads, hi, out).astype(jnp.bfloat16)


def unpack_stat(block, heads):
    x = block.astype(jnp.float32)
    return x + pltpu.roll(x, 128 - heads, 1) + pltpu.roll(x, 128 - 2 * heads, 1)


def query_kernel(heads, n_ref, qa_ref, qb_ref, k_ref, v_ref, k2_ref, v2_ref, *outs):
    rows, keys, extra = qa_ref.shape[0], k_ref.shape[0], k2_ref.shape[1]
    bias = jnp.where(lax.broadcasted_iota(jnp.int32, (1, keys), 1) < n_ref[0], 0.0, NEG)
    lane = lanes(rows)
    row = lax.broadcasted_iota(jnp.int32, (rows, extra), 0)
    col = lax.broadcasted_iota(jnp.int32, (rows, extra), 1)
    for i, q_ref in enumerate((qa_ref, qb_ref)):
        seen = (col <= row + n_ref[2 + i]) & (n_ref[1] > 0)
        tops = jnp.zeros((rows, 128), jnp.float32)
        totals = jnp.ones((rows, 128), jnp.float32)
        sent_ref = outs[2] if i == 0 else outs[3]
        for h in range(heads):
            cols = slice(h * HD, (h + 1) * HD)
            at = slice(h // GROUP * HD, (h // GROUP + 1) * HD)
            q = q_ref[:, cols]
            s_parts = [
                scores(q, k_ref[:, at]) + bias,
                jnp.where(seen, scores(q, k2_ref[0, :, at]), NEG),
            ]
            m, total, o = attend(s_parts, [wide(v_ref[:, at]), wide(v2_ref[0, :, at])])
            o = o / total
            if i == 0:
                outs[0][:, cols] = o
            else:
                sent_ref[:, cols] = o.astype(sent_ref.dtype)
            tops = jnp.where(lane == h, m, tops)
            totals = jnp.where(lane == h, total, totals)
        lse = tops + jnp.log2(totals)
        if i == 0:
            outs[1][...] = lse
        else:
            sent_ref[:, heads * HD :] = pack_stat(lse, heads)


def part_shapes(rows, heads):
    return [
        jax.ShapeDtypeStruct((rows, heads * HD), jnp.float32),
        jax.ShapeDtypeStruct((rows, 128), jnp.float32),
        jax.ShapeDtypeStruct((rows, heads * HD + 128), jnp.bfloat16),
    ]


def query_call(limits, qa, qb, k, v, k2, v2):
    rows, heads = qa.shape[0], qa.shape[1] // HD
    vmem = pl.BlockSpec(memory_space=pltpu.VMEM)

    def kernel(*refs):
        query_kernel(heads, *refs[:7], refs[7], refs[8], None, refs[9])

    return pl.pallas_call(
        kernel,
        in_specs=[pl.BlockSpec(memory_space=pltpu.SMEM)] + [vmem] * 6,
        out_specs=[vmem] * 3,
        out_shape=part_shapes(rows, heads),
        compiler_params=pltpu.CompilerParams(vmem_limit_bytes=VMEM),
        cost_estimate=pl.CostEstimate(
            flops=2 * heads * rows * (k.shape[0] + rows) * HD * 8,
            bytes_accessed=2 * rows * heads * HD * 4,
            transcendentals=0,
        ),
        name="query",
    )(limits, qa, qb, k, v, k2, v2)


def weights_of(lse, other):
    top = jnp.maximum(lse, other)
    wa, wb = jnp.exp2(lse - top), jnp.exp2(other - top)
    both = wa + wb
    return wa / both, wb / both, top + jnp.log2(both)


def merged(wa, wb, o_ref, got_ref, h):
    cols = slice(h * HD, (h + 1) * HD)
    return o_ref[:, cols] * wa[:, h : h + 1] + got_ref[:, cols].astype(jnp.float32) * wb[:, h : h + 1]


def merge_kernel(heads, o_ref, lse_ref, got_ref, *outs):
    wa, wb, lse = weights_of(lse_ref[...], unpack_stat(got_ref[:, heads * HD :], heads))
    for h in range(heads):
        cols = slice(h * HD, (h + 1) * HD)
        o = merged(wa, wb, o_ref, got_ref, h)
        if len(outs) == 3:
            outs[0][:, cols] = o
        outs[-1][:, cols] = o.astype(outs[-1].dtype)
    if len(outs) == 3:
        outs[1][...] = lse
        outs[2][:, heads * HD :] = pack_stat(lse, heads)


def merge_call(o, lse, got, last):
    rows, heads = o.shape[0], o.shape[1] // HD
    vmem = pl.BlockSpec(memory_space=pltpu.VMEM)
    shapes = part_shapes(rows, heads)
    if last:
        shapes = [jax.ShapeDtypeStruct((rows, heads * HD), jnp.bfloat16)]
    return pl.pallas_call(
        functools.partial(merge_kernel, heads),
        in_specs=[vmem] * 3,
        out_specs=[vmem] * len(shapes),
        out_shape=shapes,
        compiler_params=pltpu.CompilerParams(vmem_limit_bytes=VMEM),
        cost_estimate=pl.CostEstimate(flops=1 << 20, bytes_accessed=2 << 20, transcendentals=0),
        name="merge",
    )(o, lse, got)


def project_kernel(n_ref, w_ref, mine_ref, theirs_ref, out_ref):
    rows = mine_ref.shape[0]
    for i, ref in enumerate((mine_ref, theirs_ref)):
        at = pl.ds(pl.multiple_of(n_ref[2 + i], rows), rows)
        out_ref[at, :] = jnp.dot(ref[...], w_ref[...], preferred_element_type=jnp.float32)


def project_call(limits, mine, theirs, w):
    rows = mine.shape[0]
    vmem = pl.BlockSpec(memory_space=pltpu.VMEM)
    return pl.pallas_call(
        project_kernel,
        in_specs=[pl.BlockSpec(memory_space=pltpu.SMEM)] + [vmem] * 3,
        out_specs=vmem,
        out_shape=jax.ShapeDtypeStruct((2 * rows, w.shape[1]), jnp.float32),
        compiler_params=pltpu.CompilerParams(vmem_limit_bytes=VMEM),
        cost_estimate=pl.CostEstimate(
            flops=4 * rows * w.shape[0] * w.shape[1], bytes_accessed=3 << 20, transcendentals=0
        ),
        name="project",
    )(limits, w, mine, theirs)


def runs(total, shares):
    whole, at, out = sum(shares), 0, []
    for i in range(len(shares)):
        end = total * sum(shares[: i + 1]) // whole
        out.append((at, end))
        at = end
    return out


def per_device(
    grid,
    ctx_q,
    ctx_k,
    ctx_v,
    query_q,
    query_k,
    query_v,
    out_weight,
    anchor_index,
    owner_index,
    counts,
):
    rows = ctx_q.shape[0]
    heads = ctx_q.shape[1] // HD
    me, hid = lax.axis_index("blk"), lax.axis_index("head")
    anchor, owner = anchor_index[0], owner_index[0]
    my_code = code_of(me)
    f32 = jnp.float32

    odd = (hid & 1) == 1

    def side_of(step):
        return (my_code >> grid.bit(step, odd)) & 1

    def is_far(root, step):
        return ((code_of(root) ^ my_code) >> grid.bit(step, odd)) & 1 == 1

    def hop(x, step):
        return grid.hop(x, step)

    def cut(x, first):
        sizes = (x.shape[0] // 2, x.shape[1])
        zero = jnp.zeros((), first.dtype)
        return lax.dynamic_slice(x, (first, zero), sizes, allow_negative_indices=False)

    side, side1 = side_of(0), side_of(1)
    query = query_q[0]
    got = hop(cut(query, (1 - side) * (query.shape[0] // 2)), 0)

    q_rows, part = query.shape[0] // 2, rows // 4
    places = [part * side1, part * (1 - side1)]
    in_view = jnp.where(me == anchor, 0, counts[anchor])
    table = jnp.stack(
        [
            counts[me],
            (me == owner).astype(jnp.int32),
            side * q_rows,
            (1 - side) * q_rows,
            in_view - 2 * part * side,
            *places,
            in_view - 2 * part * (1 - side),
            *places,
            in_view,
            *[2 * part * s0 + x for s0 in (side, 1 - side) for x in places],
        ]
    )
    q_far = [is_far(owner, step) for step in range(grid.dims)]
    a_far = [is_far(anchor, step) for step in range(grid.dims)]
    half = rows // 2
    firsts = [side * q_rows, side * half, (1 - side) * half, side1 * part, (1 - side1) * part]
    firsts, table, q_far, a_far, odd, query, ctx_q, ctx_k, ctx_v = lax.optimization_barrier(
        (firsts, table, q_far, a_far, odd, query, ctx_q, ctx_k, ctx_v)
    )

    last = grid.dims - 1
    qa = jnp.where(q_far[0], got, cut(query, firsts[0]))
    for step in range(1, grid.dims):
        qa = jnp.where(q_far[step], hop(qa, step), qa)
    qb = hop(qa, 0)

    def both(cutter):
        return jnp.concatenate([cutter(ctx_k), cutter(ctx_v)], axis=1)

    mine = jnp.where(
        a_far[0],
        hop(both(lambda x: cut(x, firsts[2])), 0),
        both(lambda x: cut(x, firsts[1])),
    )
    mine = jnp.where(a_far[1], hop(cut(mine, firsts[4]), 1), cut(mine, firsts[3]))
    for step in range(2, grid.dims):
        mine = jnp.where(a_far[step], hop(mine, step), mine)
    mine = jnp.concatenate([mine, hop(mine, 1)], axis=0)
    halves = [mine, hop(mine, 0)]

    state = None
    for a, b in runs(heads, (2, 2, 2, 2)):
        state = own_call(ctx_q, ctx_k, ctx_v, state, a, b)

    o, lse, sent = query_call(table, qa, qb, ctx_k, ctx_v, query_k, query_v)
    for step in range(grid.dims):
        got = hop(sent, step)
        done = merge_call(o, lse, got, step == last)
        if step < last:
            o, lse, sent = done
    theirs = hop(done[0], 0)
    partial = project_call(table, done[0], theirs, out_weight)

    top = partial.shape[0] // 2
    low, high = partial[:top], partial[top:]
    keep, give = jnp.where(odd, high, low), jnp.where(odd, low, high)
    got = grid.head_hop(give, 0)
    total = keep + got
    for bit in range(1, log2_of(grid.n_head)):
        sent = total.astype(jnp.bfloat16)
        got = grid.head_hop(sent, bit)
        total = sent.astype(f32) + got.astype(f32)
    ours = total.astype(jnp.bfloat16)
    rest = grid.head_hop(ours, 0)
    answer = jnp.where(
        odd, jnp.concatenate([rest, ours], axis=0), jnp.concatenate([ours, rest], axis=0)
    )

    cuts = runs(heads, (2, 2, 3, 1))
    early = (cuts[0][0], cuts[1][1])
    state = anchor_call(table, 4, ctx_q, halves[:1], state, *early)
    out = None
    for a, b in cuts[2:]:
        (out,) = anchor_call(table, 10, ctx_q, halves, state, a, b, final=True, out=out)
    for a, b in cuts[:2]:
        (out,) = anchor_call(
            table, 7, ctx_q, halves[1:], state, a, b, final=True, out=out
        )
    return out, answer


def solution(mesh):
    placed = (
        P("blk", "head"),
        P("blk", "head"),
        P("blk", "head"),
        P("blk", None, "head"),
        P("blk", None, "head"),
        P("blk", None, "head"),
        P("head", "blk"),
        P(),
        P(),
        P(),
    )
    grid = Grid(mesh.shape["blk"], mesh.shape["head"])

    def whole(*args):
        return per_device(grid, *args)

    return jax.shard_map(
        whole,
        mesh=mesh,
        in_specs=placed,
        out_specs=(P("blk", "head"), P(None, "blk")),
        check_vma=False,
    )
```
